512 devices in a mesh: space: 64 (over x_lo, z, core), iter: 8 (over y, x_hi).
Axes of the slice: x: 4 (x_hi: 2, x_lo: 2; x = x_hi * 2 + x_lo), y: 4, z: 16, core: 2. Of those that a mesh axis runs over, the one named last changes fastest.
Arguments:
- start_state: float32 [8, 2, 256, 128, 128], P('iter', None, 'space'), may hold values from -1 to 1
- prior_path: float32 [8, 5, 256, 128, 128], P('iter', None, 'space'), may hold values from -1 to 1
- wave_speed: float32 [256, 128, 128], P('space'), may hold values from 0.3 to 1
- kerr_coeff: float32 [256, 128, 128], P('space'), may hold values from 0.02 to 0.15
Outputs:
- final_state: float32 [8, 2, 256, 128, 128], P('iter', None, 'space')
The draws below stay inside these ranges and needn't reach their ends.
All inputs are finite; a program needn't handle non-finite values.
Results may differ from the reference program's by a relative error of at most 0.00002.
Values sent between devices are 32-bit elements; how exact they have to be, the bound alone decides.
A program may use at most 64 MiB of HBM per device.

```python
import math
import jax
import jax.numpy as jnp
from jax import lax

CZ = 4
CX = 128
CY = 128
STEPS = 5
TICKS = 4
LANES = 8
NZ = 256
N_SPACE = 64


def steps_of(rng, dims, shards, least, high):
    loudness = 1.0
    for position, shards_of in shards:
        draws = jax.random.uniform(jax.random.fold_in(jax.random.fold_in(rng, 6), position), (shards_of,), jnp.float32, least / len(shards), high / len(shards))
        loudness = loudness * jnp.repeat(jnp.exp(draws), dims[position] // shards_of).reshape((-1,) + (1,) * (len(dims) - 1 - position))
    return loudness


def setup_inputs(seed: int = 0) -> dict:
    arg_keys = jax.random.split(jax.random.key(seed), 5)
    start_state = jnp.clip(jax.random.uniform(arg_keys[0], (LANES, 2, NZ, CX, CY), jnp.float32, -1.0, 1.0) * steps_of(arg_keys[0], (LANES, 2, NZ, CX, CY), ((0, 8), (2, 64)), -0.4, 0.0), -1.0, 1.0)
    prior_path = jnp.clip(jax.random.uniform(arg_keys[1], (LANES, STEPS, NZ, CX, CY), jnp.float32, -1.0, 1.0) * steps_of(arg_keys[1], (LANES, STEPS, NZ, CX, CY), ((0, 8), (2, 64)), -0.4, 0.0), -1.0, 1.0)
    wave_speed = jnp.clip(0.3 + 0.7 * jax.random.uniform(arg_keys[2], (NZ, CX, CY), jnp.float32) ** steps_of(arg_keys[2], (NZ, CX, CY), ((0, 64),), -0.2, 0.2), 0.3, 1.0)
    kerr_coeff = jnp.clip(jnp.exp(math.log(0.15) - 2.014903 * jax.random.uniform(arg_keys[3], (NZ, CX, CY), jnp.float32) ** steps_of(arg_keys[3], (NZ, CX, CY), ((0, 64),), -0.2, 0.2)), 0.02, 0.15)
    return dict(start_state=start_state, prior_path=prior_path, wave_speed=wave_speed, kerr_coeff=kerr_coeff)


TIME_STEP_SQ = 0.12


def pad_axis(field, along_axis):
    widths = [(0, 0)] * field.ndim
    widths[along_axis % field.ndim] = (2, 2)
    return jnp.pad(field, widths)


def second_diff(padded, along_axis):
    axis_pos = along_axis % padded.ndim
    inner_size = padded.shape[axis_pos] - 4

    def planes(offset):
        return lax.slice_in_dim(padded, offset, offset + inner_size, axis=axis_pos)

    return (-planes(0) + 16.0 * planes(1) - 30.0 * planes(2) + 16.0 * planes(3) - planes(4)) / 12.0


def leap_step(previous, current, lower_rim, upper_rim, wave_speed, kerr_coeff, guide_field):
    column = jnp.concatenate([lower_rim, current, upper_rim], axis=current.ndim - 3)
    laplace = second_diff(column, -3) + second_diff(pad_axis(current, -2), -2) + second_diff(pad_axis(current, -1), -1)
    square = guide_field * guide_field
    nonlinear = 3.0 * square * current - 2.0 * square * guide_field
    return 2.0 * current - previous + TIME_STEP_SQ * (wave_speed * laplace - kerr_coeff * nonlinear)


def reference(start_state, prior_path, wave_speed, kerr_coeff):
    lane_count = start_state.shape[0]
    speed_blocks = wave_speed.reshape(N_SPACE, CZ, CX, CY)
    kerr_blocks = kerr_coeff.reshape(N_SPACE, CZ, CX, CY)

    def one_lane(lane_args):
        lane_prev, lane_cur, lane_path = lane_args

        def one_step(carry, guide_flat):
            previous, current = carry
            guide_blocks = guide_flat.reshape(N_SPACE, CZ, CX, CY)
            zero_rim = jnp.zeros_like(guide_blocks[:1, :2])
            lower_rim = jnp.concatenate([zero_rim, guide_blocks[:-1, CZ - 2:]], 0)
            upper_rim = jnp.concatenate([guide_blocks[1:, :2], zero_rim], 0)
            fresh = leap_step(previous, current, lower_rim, upper_rim, speed_blocks, kerr_blocks, guide_blocks)
            return (current, fresh), current.reshape(NZ, CX, CY)

        start_prev = lane_prev.reshape(N_SPACE, CZ, CX, CY)
        start_cur = lane_cur.reshape(N_SPACE, CZ, CX, CY)
        (end_prev, end_cur), produced = lax.scan(one_step, (start_prev, start_cur), lane_path)
        return end_prev.reshape(NZ, CX, CY), end_cur.reshape(NZ, CX, CY), produced

    def one_tick(carry, unused):
        previous, current, incoming = carry
        previous, current, produced = lax.map(one_lane, (previous, current, incoming))
        return (previous, current, jnp.roll(produced, 1, axis=0)), None

    start_carry = (start_state[:, 0], start_state[:, 1], prior_path)
    (previous, current, incoming), unused = lax.scan(one_tick, start_carry, None, length=TICKS)
    return jnp.stack([previous, current], 1)
```

```python
import jax
import jax.numpy as jnp
from jax import lax
from jax.sharding import PartitionSpec as P

STEPS = 5
TICKS = 4
TIME_STEP_SQ = 0.12


def halo_of(path):
    count = lax.axis_size("space")
    forward = [(i, i + 1) for i in range(count - 1)]
    backward = [(t, s) for s, t in forward]
    low = lax.ppermute(path[:, -2:], "space", forward)
    high = lax.ppermute(path[:, :2], "space", backward)
    return low, high


def shift_lanes(block, distance):
    n = lax.axis_size("iter")
    return lax.ppermute(block, "iter", [(i, (i + distance) % n) for i in range(n)])


def pad_axis(field, along_axis):
    widths = [(0, 0)] * field.ndim
    widths[along_axis % field.ndim] = (2, 2)
    return jnp.pad(field, widths)


def second_diff(padded, along_axis):
    axis_pos = along_axis % padded.ndim
    inner_size = padded.shape[axis_pos] - 4

    def planes(offset):
        return lax.slice_in_dim(padded, offset, offset + inner_size, axis=axis_pos)

    return (-planes(0) + 16.0 * planes(1) - 30.0 * planes(2) + 16.0 * planes(3) - planes(4)) / 12.0


def leap_step(previous, current, lower_rim, upper_rim, wave_speed, kerr_coeff, guide_field):
    column = jnp.concatenate([lower_rim, current, upper_rim], axis=current.ndim - 3)
    laplace = (
        second_diff(column, -3)
        + second_diff(pad_axis(current, -2), -2)
        + second_diff(pad_axis(current, -1), -1)
    )
    square = guide_field * guide_field
    nonlinear = 3.0 * square * current - 2.0 * square * guide_field
    return 2.0 * current - previous + TIME_STEP_SQ * (wave_speed * laplace - kerr_coeff * nonlinear)


def per_device(start_state, prior_path, wave_speed, kerr_coeff):
    state = start_state[0]
    incoming = prior_path[0]
    low, high = halo_of(incoming)
    for tick in range(TICKS):
        previous, current = state[0], state[1]
        produced = []
        for n in range(STEPS):
            produced.append(current)
            fresh = leap_step(previous, current, low[n], high[n], wave_speed, kerr_coeff, incoming[n])
            previous, current = current, fresh
        state = jnp.stack([previous, current], 0)
        if tick + 1 < TICKS:
            incoming = jnp.stack(produced, 0)
            low, high = halo_of(incoming)
            state = shift_lanes(state, -1)
    return shift_lanes(state, TICKS - 1)[None]


def solution(mesh):
    return jax.shard_map(
        per_device,
        mesh=mesh,
        in_specs=(
            P("iter", None, "space", None, None),
            P("iter", None, "space", None, None),
            P("space", None, None),
            P("space", None, None),
        ),
        out_specs=P("iter", None, "space", None, None),
        check_vma=False,
    )
```

```python
import functools

import jax
import jax.numpy as jnp
from jax import lax
from jax.experimental import pallas as pl
from jax.experimental.pallas import tpu as pltpu
from jax.sharding import PartitionSpec as P

STEPS = 5
TICKS = 4
TIME_STEP_SQ = 0.12
ROWS = 128
PAD = 8
LAG = 8
MESH = pl.DeviceIdType.MESH

FIRST_BOUNDS = (0, 32, 64, 96, 128)
BOUNDS = (
    (0, 32, 64, 96, 128),
    (0, 24, 56, 88, 128),
    (0, 16, 48, 88, 128),
    (0, 8, 48, 88, 128),
    (0, 8, 48, 88, 128),
)
CHUNKS = 4


def emitted(window, arrived):
    return ROWS if arrived == ROWS else max(0, arrived - STEPS * LAG)


class Place:
    def __init__(self, nz):
        s, i = lax.axis_index("space"), lax.axis_index("iter")
        self.nz = nz
        self.core = lax.rem(s, 2)
        self.z = lax.rem(lax.div(s, 2), nz)
        x_lo = lax.div(s, 2 * nz)
        self.y = lax.div(i, 2)
        self.x = 2 * lax.rem(i, 2) + x_lo
        self.s, self.i = s, i
        self.dir = 1 - 2 * self.core

    def at(self, dx, dy):
        x = lax.rem(self.x + dx + 8, 4)
        y = lax.rem(self.y + dy + 8, 4)
        return {
            "space": lax.rem(x, 2) * 2 * self.nz + self.z * 2 + self.core,
            "iter": y * 2 + lax.div(x, 2),
        }

    def hi(self, dx):
        return lax.div(lax.rem(self.x + dx + 8, 4), 2)

    def dy_back(self, h):
        return 0, h - 1

    def dy_home(self, h):
        c = self.core
        first = h * (1 - 2 * c) + (1 - h) * (1 - c)
        second = h * (1 - 2 * c) + (1 - h) * c
        return first, second

    def routes(self, dys):
        d = self.dir
        h = self.hi(0)
        first_to = self.at(d, dys(h)[0])
        h_in = self.hi(-d)
        first_from = self.at(-d, -dys(h_in)[0])
        second_to = self.at(d, dys(h_in)[1])
        second_from = self.at(-d, -dys(1 - h)[1])
        return first_to, first_from, second_to, second_from


def kernel(nz, start, prior, speed, kerr, out,
           v, path0, halo, relay, wk, raw, h_send, h_recv, a_send, a_recv, b_send, b_recv, l_sem):
    me = Place(nz)
    count = 4 * nz
    back = me.routes(me.dy_back)
    home = me.routes(me.dy_home)
    up = {"space": me.s + 1}
    down = {"space": me.s - 1}

    loads = [
        pltpu.make_async_copy(speed, raw.at[0], l_sem.at[0]),
        pltpu.make_async_copy(kerr, raw.at[1], l_sem.at[1]),
        pltpu.make_async_copy(start, v.at[0, 0:2, :, pl.ds(PAD, ROWS), :], l_sem.at[2]),
        pltpu.make_async_copy(prior, path0, l_sem.at[3]),
    ]
    for load in loads:
        load.start()

    barrier = pltpu.get_barrier_semaphore()
    for writer in (back[1], back[3], home[1], home[3]):
        pl.semaphore_signal(barrier, inc=1, device_id=writer, device_id_type=MESH)

    for near in (lax.rem(me.s + 1, count), lax.rem(me.s + count - 1, count)):
        pl.semaphore_signal(barrier, inc=1, device_id={"space": near}, device_id_type=MESH)

    zero = jnp.zeros((STEPS, 4, PAD, 128), jnp.float32)
    for t in range(TICKS):
        v[t, 1:6, :, 0:PAD, :] = zero
        v[t, 1:6, :, PAD + ROWS:, :] = zero

    @pl.when(me.s == 0)
    def _():
        @pl.loop(0, TICKS * STEPS)
        def _(k):
            halo[0, k] = jnp.zeros((2, ROWS, 128), jnp.float32)

    @pl.when(me.s == count - 1)
    def _():
        @pl.loop(0, TICKS * STEPS)
        def _(k):
            halo[1, k] = jnp.zeros((2, ROWS, 128), jnp.float32)

    pl.semaphore_wait(barrier, 6)

    def halo_copy(t, j, side):
        lo, hi = BOUNDS[t][j], BOUNDS[t][j + 1]
        planes = pl.ds(2, 2) if side == 0 else pl.ds(0, 2)
        if t == 0:
            src = prior.at[:, planes, pl.ds(lo, hi - lo), :]
        else:
            src = v.at[t - 1, 1:6, planes, pl.ds(PAD + lo, hi - lo), :]
        return pltpu.make_async_remote_copy(
            src_ref=src,
            dst_ref=halo.at[side, pl.ds(STEPS * t, STEPS), :, pl.ds(lo, hi - lo), :],
            send_sem=h_send.at[t, j, side],
            recv_sem=h_recv.at[t, j, side],
            device_id=up if side == 0 else down,
            device_id_type=MESH,
        )

    def send_halo(t, j):
        @pl.when(me.s < count - 1)
        def _():
            halo_copy(t, j, 0).start()

        @pl.when(me.s > 0)
        def _():
            halo_copy(t, j, 1).start()

    def wait_halo(t, j):
        @pl.when(me.s > 0)
        def _():
            halo_copy(t, j, 0).wait_recv()

        @pl.when(me.s < count - 1)
        def _():
            halo_copy(t, j, 1).wait_recv()

    def wait_halo_sent(t, j):
        @pl.when(me.s < count - 1)
        def _():
            halo_copy(t, j, 0).wait_send()

        @pl.when(me.s > 0)
        def _():
            halo_copy(t, j, 1).wait_send()

    def first_hop(t, j):
        lo, hi = BOUNDS[t][j], BOUNDS[t][j + 1]
        return pltpu.make_async_remote_copy(
            src_ref=v.at[t - 1, 5:7, :, pl.ds(PAD + lo, hi - lo), :],
            dst_ref=relay.at[t - 1, :, :, pl.ds(lo, hi - lo), :],
            send_sem=a_send.at[t - 1, j],
            recv_sem=a_recv.at[t - 1, j],
            device_id=(back if t < TICKS else home)[0],
            device_id_type=MESH,
        )

    def second_hop(t, j):
        lo, hi = BOUNDS[t][j], BOUNDS[t][j + 1]
        if t < TICKS:
            dst = v.at[t, 0:2, :, pl.ds(PAD + lo, hi - lo), :]
        else:
            dst = out.at[:, :, pl.ds(lo, hi - lo), :]
        return pltpu.make_async_remote_copy(
            src_ref=relay.at[t - 1, :, :, pl.ds(lo, hi - lo), :],
            dst_ref=dst,
            send_sem=b_send.at[t - 1, j],
            recv_sem=b_recv.at[t - 1, j],
            device_id=(back if t < TICKS else home)[2],
            device_id_type=MESH,
        )

    for j in range(CHUNKS):
        send_halo(0, j)

    loads[0].wait()
    loads[1].wait()

    @pl.loop(0, ROWS // 8)
    def _(k):
        rows = pl.ds(pl.multiple_of(k * 8, 8), 8)
        wk[0, :, rows, :] = raw[0, :, rows, :] * (TIME_STEP_SQ / 12.0)
        wk[1, :, rows, :] = raw[1, :, rows, :] * TIME_STEP_SQ

    loads[2].wait()
    loads[3].wait()

    lane = lax.broadcasted_iota(jnp.int32, (8, 128), 1)

    def step_block(t, n, r):
        mid = pl.ds(r + PAD, 8)
        rows = pl.ds(r, 8)
        tile = lambda z, off: v[t, n + 1, z, pl.ds(r + PAD + off, 8), :]
        u = [tile(z, 0) for z in range(4)]
        col = [halo[0, STEPS * t + n, 0, rows, :], halo[0, STEPS * t + n, 1, rows, :], *u,
               halo[1, STEPS * t + n, 0, rows, :], halo[1, STEPS * t + n, 1, rows, :]]
        for z in range(4):
            c = u[z]
            above, below = v[t, n + 1, z, pl.ds(r, 8), :], v[t, n + 1, z, pl.ds(r + 2 * PAD, 8), :]
            band = jnp.concatenate([above, c, below], axis=0)
            s1 = band[7:15] + band[9:17]
            s2 = band[6:14] + band[10:18]
            s1 += col[z + 1] + col[z + 3]
            s2 += col[z] + col[z + 4]
            s1 += jnp.where(lane < 1, 0.0, pltpu.roll(c, 1, 1)) + jnp.where(lane > 126, 0.0, pltpu.roll(c, 127, 1))
            s2 += jnp.where(lane < 2, 0.0, pltpu.roll(c, 2, 1)) + jnp.where(lane > 125, 0.0, pltpu.roll(c, 126, 1))
            laplace = 16.0 * s1 - s2 - 90.0 * c
            g = path0[n, z, rows, :] if t == 0 else v[t - 1, n + 1, z, mid, :]
            kg = wk[1, z, rows, :] * (g * g)
            v[t, n + 2, z, mid, :] = (
                (2.0 * c - v[t, n, z, mid, :]) + wk[0, z, rows, :] * laplace + kg * (2.0 * g - 3.0 * c)
            )

    def step_rows(t, n, lo, hi):
        if hi <= lo:
            return

        @pl.loop(0, (hi - lo) // 8)
        def _(k):
            step_block(t, n, pl.multiple_of(lo + k * 8, 8))

    for t in range(TICKS):
        bounds = BOUNDS[t]
        sent = 0
        for j in range(CHUNKS):
            if t > 0:
                first_hop(t, j).wait_recv()
                second_hop(t, j).start()
            if t > 0:
                second_hop(t, j).wait_recv()
            wait_halo(t, j)
            lo, hi = bounds[j], bounds[j + 1]
            for n in range(STEPS):
                lag = LAG * (n + 1)
                step_rows(t, n, max(0, lo - lag), ROWS if hi == ROWS else max(0, hi - lag))
            ready = emitted(t, hi)
            while sent < CHUNKS and BOUNDS[t + 1][sent + 1] <= ready:
                first_hop(t + 1, sent).start()
                if t + 1 < TICKS:
                    send_halo(t + 1, sent)
                sent += 1
    for j in range(CHUNKS):
        first_hop(TICKS, j).wait_recv()
        second_hop(TICKS, j).start()
    for j in range(CHUNKS):
        second_hop(TICKS, j).wait_recv()
    for t in range(TICKS):
        for j in range(CHUNKS):
            wait_halo_sent(t, j)
            first_hop(t + 1, j).wait_send()
            second_hop(t + 1, j).wait_send()


def per_device(nz, start_state, prior_path, wave_speed, kerr_coeff):
    any_space = pl.BlockSpec(memory_space=pl.ANY)
    out = pl.pallas_call(
        functools.partial(kernel, nz),
        out_shape=jax.ShapeDtypeStruct((2, 4, ROWS, 128), jnp.float32),
        in_specs=[any_space] * 4,
        out_specs=any_space,
        scratch_shapes=[
            pltpu.VMEM((TICKS, 7, 4, ROWS + 2 * PAD, 128), jnp.float32),
            pltpu.VMEM((STEPS, 4, ROWS, 128), jnp.float32),
            pltpu.VMEM((2, TICKS * STEPS, 2, ROWS, 128), jnp.float32),
            pltpu.VMEM((TICKS, 2, 4, ROWS, 128), jnp.float32),
            pltpu.VMEM((2, 4, ROWS, 128), jnp.float32),
            pltpu.VMEM((2, 4, ROWS, 128), jnp.float32),
            pltpu.SemaphoreType.DMA((TICKS, CHUNKS, 2)),
            pltpu.SemaphoreType.DMA((TICKS, CHUNKS, 2)),
            pltpu.SemaphoreType.DMA((TICKS, CHUNKS)),
            pltpu.SemaphoreType.DMA((TICKS, CHUNKS)),
            pltpu.SemaphoreType.DMA((TICKS, CHUNKS)),
            pltpu.SemaphoreType.DMA((TICKS, CHUNKS)),
            pltpu.SemaphoreType.DMA((4,)),
        ],
        compiler_params=pltpu.CompilerParams(
            collective_id=0, has_side_effects=True, vmem_limit_bytes=40 << 20
        ),
        name="relaxation",
    )(start_state[0], prior_path[0], wave_speed, kerr_coeff)
    return out[None]


def solution(mesh):
    nz = mesh.shape["space"] // 4
    return jax.shard_map(
        functools.partial(per_device, nz),
        mesh=mesh,
        in_specs=(
            P("iter", None, "space", None, None),
            P("iter", None, "space", None, None),
            P("space", None, None),
            P("space", None, None),
        ),
        out_specs=P("iter", None, "space", None, None),
        check_vma=False,
    )
```

```python
import functools

import jax
import jax.numpy as jnp
from jax import lax
from jax.experimental import pallas as pl
from jax.experimental.pallas import tpu as pltpu
from jax.sharding import PartitionSpec as P

STEPS = 5
TICKS = 4
TIME_STEP_SQ = 0.12
ROWS = 128
PAD = 8
LAG = 8
MESH = pl.DeviceIdType.MESH

FIRST_BOUNDS = (0, 32, 64, 96, 128)
BOUNDS = (
    (0, 32, 64, 96, 128),
    (0, 24, 56, 88, 128),
    (0, 16, 48, 88, 128),
    (0, 8, 48, 88, 128),
    (0, 8, 48, 88, 128),
)
CHUNKS = 4


def emitted(window, arrived):
    return ROWS if arrived == ROWS else max(0, arrived - STEPS * LAG)


class Place:
    def __init__(self, nz):
        s, i = lax.axis_index("space"), lax.axis_index("iter")
        self.nz = nz
        self.core = lax.rem(s, 2)
        self.z = lax.rem(lax.div(s, 2), nz)
        x_lo = lax.div(s, 2 * nz)
        self.y = lax.div(i, 2)
        self.x = 2 * lax.rem(i, 2) + x_lo
        self.s, self.i = s, i
        self.h = lax.rem(i, 2)

    def at(self, dx, dy):
        x = lax.rem(self.x + dx + 8, 4)
        y = lax.rem(self.y + dy + 8, 4)
        return {
            "space": lax.rem(x, 2) * 2 * self.nz + self.z * 2 + self.core,
            "iter": y * 2 + lax.div(x, 2),
        }

    def back(self):
        return self.at(2, self.h - 1), self.at(2, self.h)

    def home(self):
        return self.at(2, 1 + self.h), self.at(2, self.h - 2)


def kernel(nz, start, prior, speed, kerr, out,
           v, path0, halo, wk, raw, h_send, h_recv, s_send, s_recv, l_sem):
    me = Place(nz)
    count = 4 * nz
    back = me.back()
    home = me.home()
    up = {"space": me.s + 1}
    down = {"space": me.s - 1}

    loads = [
        pltpu.make_async_copy(speed, raw.at[0], l_sem.at[0]),
        pltpu.make_async_copy(kerr, raw.at[1], l_sem.at[1]),
        pltpu.make_async_copy(start, v.at[0, 0:2, :, pl.ds(PAD, ROWS), :], l_sem.at[2]),
        pltpu.make_async_copy(prior, path0, l_sem.at[3]),
    ]
    for load in loads:
        load.start()

    barrier = pltpu.get_barrier_semaphore()
    for writer in (back[1], home[1]):
        pl.semaphore_signal(barrier, inc=1, device_id=writer, device_id_type=MESH)

    for near in (lax.rem(me.s + 1, count), lax.rem(me.s + count - 1, count)):
        pl.semaphore_signal(barrier, inc=1, device_id={"space": near}, device_id_type=MESH)

    zero = jnp.zeros((STEPS, 4, PAD, 128), jnp.float32)
    for t in range(TICKS):
        v[t, 1:6, :, 0:PAD, :] = zero
        v[t, 1:6, :, PAD + ROWS:, :] = zero

    @pl.when(me.s == 0)
    def _():
        @pl.loop(0, TICKS * STEPS)
        def _(k):
            halo[0, k] = jnp.zeros((2, ROWS, 128), jnp.float32)

    @pl.when(me.s == count - 1)
    def _():
        @pl.loop(0, TICKS * STEPS)
        def _(k):
            halo[1, k] = jnp.zeros((2, ROWS, 128), jnp.float32)

    pl.semaphore_wait(barrier, 4)

    def halo_copy(t, j, side):
        lo, hi = BOUNDS[t][j], BOUNDS[t][j + 1]
        planes = pl.ds(2, 2) if side == 0 else pl.ds(0, 2)
        if t == 0:
            src = prior.at[:, planes, pl.ds(lo, hi - lo), :]
        else:
            src = v.at[t - 1, 1:6, planes, pl.ds(PAD + lo, hi - lo), :]
        return pltpu.make_async_remote_copy(
            src_ref=src,
            dst_ref=halo.at[side, pl.ds(STEPS * t, STEPS), :, pl.ds(lo, hi - lo), :],
            send_sem=h_send.at[t, j, side],
            recv_sem=h_recv.at[t, j, side],
            device_id=up if side == 0 else down,
            device_id_type=MESH,
        )

    def send_halo(t, j):
        @pl.when(me.s < count - 1)
        def _():
            halo_copy(t, j, 0).start()

        @pl.when(me.s > 0)
        def _():
            halo_copy(t, j, 1).start()

    def wait_halo(t, j):
        @pl.when(me.s > 0)
        def _():
            halo_copy(t, j, 0).wait_recv()

        @pl.when(me.s < count - 1)
        def _():
            halo_copy(t, j, 1).wait_recv()

    def wait_halo_sent(t, j):
        @pl.when(me.s < count - 1)
        def _():
            halo_copy(t, j, 0).wait_send()

        @pl.when(me.s > 0)
        def _():
            halo_copy(t, j, 1).wait_send()

    def state_copy(t, j):
        lo, hi = BOUNDS[t][j], BOUNDS[t][j + 1]
        if t < TICKS:
            dst = v.at[t, 0:2, :, pl.ds(PAD + lo, hi - lo), :]
        else:
            dst = out.at[:, :, pl.ds(lo, hi - lo), :]
        return pltpu.make_async_remote_copy(
            src_ref=v.at[t - 1, 5:7, :, pl.ds(PAD + lo, hi - lo), :],
            dst_ref=dst,
            send_sem=s_send.at[t - 1, j],
            recv_sem=s_recv.at[t - 1, j],
            device_id=(back if t < TICKS else home)[0],
            device_id_type=MESH,
        )

    for j in range(CHUNKS):
        send_halo(0, j)

    loads[0].wait()
    loads[1].wait()

    @pl.loop(0, ROWS // 8)
    def _(k):
        rows = pl.ds(pl.multiple_of(k * 8, 8), 8)
        scaled = raw[0, :, rows, :] * (TIME_STEP_SQ / 12.0)
        wk[0, :, rows, :] = scaled
        wk[1, :, rows, :] = raw[1, :, rows, :] * (3.0 * TIME_STEP_SQ)
        wk[2, :, rows, :] = 2.0 - 90.0 * scaled

    loads[2].wait()
    loads[3].wait()

    def step_block(t, n, r, size):
        mid = pl.ds(r + PAD, size)
        rows = pl.ds(r, size)
        lane = lax.broadcasted_iota(jnp.int32, (size, 128), 1)
        k = STEPS * t + n
        col = [halo[0, k, 0, rows, :], halo[0, k, 1, rows, :],
               *[v[t, n + 1, z, mid, :] for z in range(4)],
               halo[1, k, 0, rows, :], halo[1, k, 1, rows, :]]
        for z in range(4):
            c = col[z + 2]

            def shifted(off):
                return v[t, n + 1, z, pl.ds(r + PAD + off, size), :]

            def turned(off):
                inside = lane >= off if off > 0 else lane < 128 + off
                return jnp.where(inside, pltpu.roll(c, off % 128, 1), 0.0)

            s1 = (shifted(-1) + shifted(1)) + (col[z + 1] + col[z + 3]) + (turned(-1) + turned(1))
            s2 = (shifted(-2) + shifted(2)) + (col[z] + col[z + 4]) + (turned(-2) + turned(2))
            g = path0[n, z, rows, :] if t == 0 else v[t - 1, n + 1, z, mid, :]
            v[t, n + 2, z, mid, :] = (
                (wk[2, z, rows, :] * c - v[t, n, z, mid, :])
                + wk[0, z, rows, :] * (16.0 * s1 - s2)
                + (wk[1, z, rows, :] * (g * g)) * ((2.0 / 3.0) * g - c)
            )

    def step_rows(t, n, lo, hi):
        if hi <= lo:
            return
        size = 16
        for r in range(lo, hi, size):
            step_block(t, n, r, min(size, hi - r))

    for t in range(TICKS):
        bounds = BOUNDS[t]
        sent = 0
        for j in range(CHUNKS):
            if t > 0:
                state_copy(t, j).wait_recv()
            wait_halo(t, j)
            lo, hi = bounds[j], bounds[j + 1]
            for n in range(STEPS):
                lag = LAG * (n + 1)
                step_rows(t, n, max(0, lo - lag), ROWS if hi == ROWS else max(0, hi - lag))
            ready = emitted(t, hi)
            while sent < CHUNKS and BOUNDS[t + 1][sent + 1] <= ready:
                state_copy(t + 1, sent).start()
                if t + 1 < TICKS:
                    send_halo(t + 1, sent)
                sent += 1
    for j in range(CHUNKS):
        state_copy(TICKS, j).wait_recv()
    for t in range(TICKS):
        for j in range(CHUNKS):
            wait_halo_sent(t, j)
            state_copy(t + 1, j).wait_send()


def per_device(nz, start_state, prior_path, wave_speed, kerr_coeff):
    any_space = pl.BlockSpec(memory_space=pl.ANY)
    out = pl.pallas_call(
        functools.partial(kernel, nz),
        out_shape=jax.ShapeDtypeStruct((2, 4, ROWS, 128), jnp.float32),
        in_specs=[any_space] * 4,
        out_specs=any_space,
        scratch_shapes=[
            pltpu.VMEM((TICKS, 7, 4, ROWS + 2 * PAD, 128), jnp.float32),
            pltpu.VMEM((STEPS, 4, ROWS, 128), jnp.float32),
            pltpu.VMEM((2, TICKS * STEPS, 2, ROWS, 128), jnp.float32),
            pltpu.VMEM((3, 4, ROWS, 128), jnp.float32),
            pltpu.VMEM((2, 4, ROWS, 128), jnp.float32),
            pltpu.SemaphoreType.DMA((TICKS, CHUNKS, 2)),
            pltpu.SemaphoreType.DMA((TICKS, CHUNKS, 2)),
            pltpu.SemaphoreType.DMA((TICKS, CHUNKS)),
            pltpu.SemaphoreType.DMA((TICKS, CHUNKS)),
            pltpu.SemaphoreType.DMA((4,)),
        ],
        compiler_params=pltpu.CompilerParams(
            collective_id=0, has_side_effects=True, vmem_limit_bytes=62 << 20
        ),
        name="relaxation",
    )(start_state[0], prior_path[0], wave_speed, kerr_coeff)
    return out[None]


def solution(mesh):
    nz = mesh.shape["space"] // 4
    return jax.shard_map(
        functools.partial(per_device, nz),
        mesh=mesh,
        in_specs=(
            P("iter", None, "space", None, None),
            P("iter", None, "space", None, None),
            P("space", None, None),
            P("space", None, None),
        ),
        out_specs=P("iter", None, "space", None, None),
        check_vma=False,
    )
```

```python
import functools

import jax
import jax.numpy as jnp
from jax import lax
from jax.experimental import pallas as pl
from jax.experimental.pallas import tpu as pltpu
from jax.sharding import PartitionSpec as P

STEPS = 5
TICKS = 4
TIME_STEP_SQ = 0.12
ROWS = 128
PAD = 8
LAG = 2
MESH = pl.DeviceIdType.MESH

BOUNDS = (
    (0, 32, 64, 96, 128),
    (0, 16, 48, 80, 128),
    (0, 32, 64, 96, 128),
    (0, 16, 48, 80, 128),
    (0, 32, 64, 96, 128),
)
CHUNKS = 4
FORWARD_AFTER = 2


def emitted(window, arrived):
    return ROWS if arrived == ROWS else max(0, arrived - STEPS * LAG) // 8 * 8


class Place:
    def __init__(self, nz):
        s, i = lax.axis_index("space"), lax.axis_index("iter")
        self.nz = nz
        self.core = lax.rem(s, 2)
        self.z = lax.rem(lax.div(s, 2), nz)
        x_lo = lax.div(s, 2 * nz)
        self.y = lax.div(i, 2)
        self.x = 2 * lax.rem(i, 2) + x_lo
        self.s, self.i = s, i
        self.h = lax.rem(i, 2)

    def at(self, dx, dy):
        x = lax.rem(self.x + dx + 8, 4)
        y = lax.rem(self.y + dy + 8, 4)
        return {
            "space": lax.rem(x, 2) * 2 * self.nz + self.z * 2 + self.core,
            "iter": y * 2 + lax.div(x, 2),
        }

    def back(self):
        return self.at(2, self.h - 1), self.at(2, self.h)

    def home(self):
        return self.at(2, 1 + self.h), self.at(2, self.h - 2)


def kernel(nz, start, prior, speed, kerr, out,
           v, path0, halo, passing, wk, raw, h_send, h_recv, s_send, s_recv, p_send, p_recv, l_sem):
    me = Place(nz)
    count = 4 * nz
    back = me.back()
    home = me.home()
    up = {"space": me.s + 1}
    down = {"space": me.s - 1}
    half = count // 2
    last = nz - 1
    ends = (half - 1, half)
    passers = (
        [half + 2 * z for z in (last, 1, last - 1)],
        [1 + 2 * z for z in (0, 1, last - 1)],
    )

    loads = [
        pltpu.make_async_copy(speed, raw.at[0], l_sem.at[0]),
        pltpu.make_async_copy(kerr, raw.at[1], l_sem.at[1]),
        pltpu.make_async_copy(start, v.at[0, 0:2, :, pl.ds(PAD, ROWS), :], l_sem.at[2]),
        pltpu.make_async_copy(prior, path0, l_sem.at[3]),
    ]
    for load in loads:
        load.start()

    barrier = pltpu.get_barrier_semaphore()
    for writer in (back[1], home[1]):
        pl.semaphore_signal(barrier, inc=1, device_id=writer, device_id_type=MESH)

    for near in (lax.rem(me.s + 1, count), lax.rem(me.s + count - 1, count)):
        pl.semaphore_signal(barrier, inc=1, device_id={"space": near}, device_id_type=MESH)

    for side in range(2):
        for passer in passers[side]:
            @pl.when(me.s == passer)
            def _():
                pl.semaphore_signal(barrier, inc=1, device_id={"space": ends[side]}, device_id_type=MESH)

            @pl.when(me.s == ends[1 - side])
            def _():
                pl.semaphore_signal(barrier, inc=1, device_id={"space": passer}, device_id_type=MESH)

    zero = jnp.zeros((STEPS, 4, PAD, 128), jnp.float32)
    for t in range(TICKS):
        v[t, 1:6, :, 0:PAD, :] = zero
        v[t, 1:6, :, PAD + ROWS:, :] = zero

    @pl.when(me.s == 0)
    def _():
        @pl.loop(0, TICKS * STEPS)
        def _(k):
            halo[0, k] = jnp.zeros((2, ROWS, 128), jnp.float32)

    @pl.when(me.s == count - 1)
    def _():
        @pl.loop(0, TICKS * STEPS)
        def _(k):
            halo[1, k] = jnp.zeros((2, ROWS, 128), jnp.float32)

    peers = jnp.int32(4)
    for side in range(2):
        peers += 3 * (me.s == ends[side]).astype(jnp.int32)
        for passer in passers[side]:
            peers += (me.s == passer).astype(jnp.int32)
    pl.semaphore_wait(barrier, peers)

    def halo_copy(t, j, side):
        lo, hi = BOUNDS[t][j], BOUNDS[t][j + 1]
        planes = pl.ds(2, 2) if side == 0 else pl.ds(0, 2)
        if t == 0:
            src = prior.at[:, planes, pl.ds(lo, hi - lo), :]
        else:
            src = v.at[t - 1, 1:6, planes, pl.ds(PAD + lo, hi - lo), :]
        return pltpu.make_async_remote_copy(
            src_ref=src,
            dst_ref=halo.at[side, pl.ds(STEPS * t, STEPS), :, pl.ds(lo, hi - lo), :],
            send_sem=h_send.at[t, j, side],
            recv_sem=h_recv.at[t, j, side],
            device_id=up if side == 0 else down,
            device_id_type=MESH,
        )

    def pass_in(t, j, side):
        lo, hi = BOUNDS[t][j], BOUNDS[t][j + 1]
        return pltpu.make_async_remote_copy(
            src_ref=v.at[t - 1, 1:6, pl.ds(2 - 2 * side, 2), pl.ds(PAD + lo, hi - lo), :],
            dst_ref=passing.at[t - 1, :, :, pl.ds(lo, hi - lo), :],
            send_sem=h_send.at[t, j, side],
            recv_sem=p_recv.at[t - 1, j],
            device_id={"space": passers[side][j - 1]},
            device_id_type=MESH,
        )

    def pass_out(t, j, side):
        lo, hi = BOUNDS[t][j], BOUNDS[t][j + 1]
        return pltpu.make_async_remote_copy(
            src_ref=passing.at[t - 1, :, :, pl.ds(lo, hi - lo), :],
            dst_ref=halo.at[side, pl.ds(STEPS * t, STEPS), :, pl.ds(lo, hi - lo), :],
            send_sem=p_send.at[t - 1, j],
            recv_sem=h_recv.at[t, j, side],
            device_id={"space": ends[1 - side]},
            device_id_type=MESH,
        )

    def forward(t, j):
        for side in range(2):
            @pl.when(me.s == passers[side][j - 1])
            def _():
                pass_in(t, j, side).wait_recv()
                pass_out(t, j, side).start()

    def wait_forwarded(t, j):
        for side in range(2):
            @pl.when(me.s == passers[side][j - 1])
            def _():
                pass_out(t, j, side).wait_send()

    def send_halo(t, j):
        roundabout = t > 0 and j > 0
        for side, near in ((0, me.s < count - 1), (1, me.s > 0)):
            if roundabout:
                near = near & (me.s != ends[side])

                @pl.when(me.s == ends[side])
                def _():
                    pass_in(t, j, side).start()

            @pl.when(near)
            def _():
                halo_copy(t, j, side).start()

    def wait_halo(t, j):
        @pl.when(me.s > 0)
        def _():
            halo_copy(t, j, 0).wait_recv()

        @pl.when(me.s < count - 1)
        def _():
            halo_copy(t, j, 1).wait_recv()

    def wait_halo_sent(t, j):
        @pl.when(me.s < count - 1)
        def _():
            halo_copy(t, j, 0).wait_send()

        @pl.when(me.s > 0)
        def _():
            halo_copy(t, j, 1).wait_send()

    def state_copy(t, j):
        lo, hi = BOUNDS[t][j], BOUNDS[t][j + 1]
        if t < TICKS:
            dst = v.at[t, 0:2, :, pl.ds(PAD + lo, hi - lo), :]
        else:
            dst = out.at[:, :, pl.ds(lo, hi - lo), :]
        return pltpu.make_async_remote_copy(
            src_ref=v.at[t - 1, 5:7, :, pl.ds(PAD + lo, hi - lo), :],
            dst_ref=dst,
            send_sem=s_send.at[t - 1, j],
            recv_sem=s_recv.at[t - 1, j],
            device_id=(back if t < TICKS else home)[0],
            device_id_type=MESH,
        )

    for j in range(CHUNKS):
        send_halo(0, j)

    loads[0].wait()
    loads[1].wait()

    @pl.loop(0, ROWS // 8)
    def _(k):
        rows = pl.ds(pl.multiple_of(k * 8, 8), 8)
        scaled = raw[0, :, rows, :] * (TIME_STEP_SQ / 12.0)
        wk[0, :, rows, :] = scaled
        wk[1, :, rows, :] = raw[1, :, rows, :] * (3.0 * TIME_STEP_SQ)
        wk[2, :, rows, :] = 2.0 - 90.0 * scaled

    loads[2].wait()
    loads[3].wait()

    def step_block(t, n, r, size):
        mid = pl.ds(r + PAD, size)
        rows = pl.ds(r, size)
        lane = lax.broadcasted_iota(jnp.int32, (size, 128), 1)
        k = STEPS * t + n
        col = [halo[0, k, 0, rows, :], halo[0, k, 1, rows, :],
               *[v[t, n + 1, z, mid, :] for z in range(4)],
               halo[1, k, 0, rows, :], halo[1, k, 1, rows, :]]
        for z in range(4):
            c = col[z + 2]

            def shifted(off):
                return v[t, n + 1, z, pl.ds(r + PAD + off, size), :]

            def turned(off):
                inside = lane >= off if off > 0 else lane < 128 + off
                return jnp.where(inside, pltpu.roll(c, off % 128, 1), 0.0)

            s1 = (shifted(-1) + shifted(1)) + (col[z + 1] + col[z + 3]) + (turned(-1) + turned(1))
            s2 = (shifted(-2) + shifted(2)) + (col[z] + col[z + 4]) + (turned(-2) + turned(2))
            g = path0[n, z, rows, :] if t == 0 else v[t - 1, n + 1, z, mid, :]
            v[t, n + 2, z, mid, :] = (
                (wk[2, z, rows, :] * c - v[t, n, z, mid, :])
                + wk[0, z, rows, :] * (16.0 * s1 - s2)
                + (wk[1, z, rows, :] * (g * g)) * ((2.0 / 3.0) * g - c)
            )

    def step_rows(t, n, lo, hi):
        if hi <= lo:
            return
        size = 16
        for r in range(lo, hi, size):
            step_block(t, n, r, min(size, hi - r))

    forwards = []
    for t in range(TICKS):
        bounds = BOUNDS[t]
        sent = 0
        for j in range(CHUNKS):
            event = CHUNKS * t + j
            while forwards and forwards[0][0] + FORWARD_AFTER <= event:
                forward(*forwards.pop(0)[1:])
            if t > 0:
                state_copy(t, j).wait_recv()
            wait_halo(t, j)
            lo, hi = bounds[j], bounds[j + 1]
            for n in range(STEPS):
                lag = LAG * (n + 1)
                step_rows(t, n, max(0, lo - lag), ROWS if hi == ROWS else max(0, hi - lag))
            ready = emitted(t, hi)
            while sent < CHUNKS and BOUNDS[t + 1][sent + 1] <= ready:
                state_copy(t + 1, sent).start()
                if t + 1 < TICKS:
                    send_halo(t + 1, sent)
                    if sent:
                        forwards.append((event, t + 1, sent))
                sent += 1
    for j in range(CHUNKS):
        state_copy(TICKS, j).wait_recv()
    for t in range(TICKS):
        for j in range(CHUNKS):
            wait_halo_sent(t, j)
            if t and j:
                wait_forwarded(t, j)
            state_copy(t + 1, j).wait_send()


def per_device(nz, start_state, prior_path, wave_speed, kerr_coeff):
    any_space = pl.BlockSpec(memory_space=pl.ANY)
    out = pl.pallas_call(
        functools.partial(kernel, nz),
        out_shape=jax.ShapeDtypeStruct((2, 4, ROWS, 128), jnp.float32),
        in_specs=[any_space] * 4,
        out_specs=any_space,
        scratch_shapes=[
            pltpu.VMEM((TICKS, 7, 4, ROWS + 2 * PAD, 128), jnp.float32),
            pltpu.VMEM((STEPS, 4, ROWS, 128), jnp.float32),
            pltpu.VMEM((2, TICKS * STEPS, 2, ROWS, 128), jnp.float32),
            pltpu.VMEM((TICKS - 1, STEPS, 2, ROWS, 128), jnp.float32),
            pltpu.VMEM((3, 4, ROWS, 128), jnp.float32),
            pltpu.VMEM((2, 4, ROWS, 128), jnp.float32),
            pltpu.SemaphoreType.DMA((TICKS, CHUNKS, 2)),
            pltpu.SemaphoreType.DMA((TICKS, CHUNKS, 2)),
            pltpu.SemaphoreType.DMA((TICKS, CHUNKS)),
            pltpu.SemaphoreType.DMA((TICKS, CHUNKS)),
            pltpu.SemaphoreType.DMA((TICKS - 1, CHUNKS)),
            pltpu.SemaphoreType.DMA((TICKS - 1, CHUNKS)),
            pltpu.SemaphoreType.DMA((4,)),
        ],
        compiler_params=pltpu.CompilerParams(
            collective_id=0, has_side_effects=True, vmem_limit_bytes=62 << 20
        ),
        name="relaxation",
    )(start_state[0], prior_path[0], wave_speed, kerr_coeff)
    return out[None]


def solution(mesh):
    nz = mesh.shape["space"] // 4
    return jax.shard_map(
        functools.partial(per_device, nz),
        mesh=mesh,
        in_specs=(
            P("iter", None, "space", None, None),
            P("iter", None, "space", None, None),
            P("space", None, None),
            P("space", None, None),
        ),
        out_specs=P("iter", None, "space", None, None),
        check_vma=False,
    )
```

```python
import functools

import jax
import jax.numpy as jnp
from jax import lax
from jax.experimental import pallas as pl
from jax.experimental.pallas import tpu as pltpu
from jax.sharding import PartitionSpec as P

STEPS = 5
TICKS = 4
TIME_STEP_SQ = 0.12
ROWS = 128
PAD = 8
LAG = 2
MESH = pl.DeviceIdType.MESH

CHUNKS = 8
BOUNDS = (tuple(range(0, ROWS + 1, ROWS // CHUNKS)),) * (TICKS + 1)
FORWARD_AFTER = 3


def emitted(window, arrived):
    return ROWS if arrived == ROWS else max(0, arrived - STEPS * LAG) // 8 * 8


class Place:
    def __init__(self, nz):
        s, i = lax.axis_index("space"), lax.axis_index("iter")
        self.nz = nz
        self.core = lax.rem(s, 2)
        self.z = lax.rem(lax.div(s, 2), nz)
        x_lo = lax.div(s, 2 * nz)
        self.y = lax.div(i, 2)
        self.x = 2 * lax.rem(i, 2) + x_lo
        self.s, self.i = s, i
        self.h = lax.rem(i, 2)

    def at(self, dx, dy):
        x = lax.rem(self.x + dx + 8, 4)
        y = lax.rem(self.y + dy + 8, 4)
        return {
            "space": lax.rem(x, 2) * 2 * self.nz + self.z * 2 + self.core,
            "iter": y * 2 + lax.div(x, 2),
        }

    def back(self):
        return self.at(2, self.h - 1), self.at(2, self.h)

    def home(self):
        return self.at(2, 1 + self.h), self.at(2, self.h - 2)


def kernel(nz, start, prior, speed, kerr, out_prev, out_cur,
           v, path0, halo, passing, wk, raw, h_send, h_recv, s_send, s_recv, p_send, p_recv, l_sem):
    me = Place(nz)
    count = 4 * nz
    back = me.back()
    home = me.home()
    up = {"space": me.s + 1}
    down = {"space": me.s - 1}
    half = count // 2
    last = nz - 1
    ends = (half - 1, half)
    passers = (
        [half + 2 * z for z in (last, 1, last - 1, 2, last - 2, 3, last - 3)],
        [1 + 2 * z for z in (0, 1, last - 1, 2, last - 2, 3, last - 3)],
    )

    loads = [
        pltpu.make_async_copy(speed, raw.at[0], l_sem.at[0]),
        pltpu.make_async_copy(kerr, raw.at[1], l_sem.at[1]),
        pltpu.make_async_copy(start, v.at[0, 0:2, :, pl.ds(PAD, ROWS), :], l_sem.at[2]),
        pltpu.make_async_copy(prior, path0, l_sem.at[3]),
    ]
    for load in loads:
        load.start()

    barrier = pltpu.get_barrier_semaphore()
    for writer in (back[1], home[1]):
        pl.semaphore_signal(barrier, inc=1, device_id=writer, device_id_type=MESH)

    for near in (lax.rem(me.s + 1, count), lax.rem(me.s + count - 1, count)):
        pl.semaphore_signal(barrier, inc=1, device_id={"space": near}, device_id_type=MESH)

    for side in range(2):
        for passer in passers[side]:
            @pl.when(me.s == passer)
            def _():
                pl.semaphore_signal(barrier, inc=1, device_id={"space": ends[side]}, device_id_type=MESH)

            @pl.when(me.s == ends[1 - side])
            def _():
                pl.semaphore_signal(barrier, inc=1, device_id={"space": passer}, device_id_type=MESH)

    zero = jnp.zeros((STEPS, 4, PAD, 128), jnp.float32)
    for t in range(TICKS):
        v[t, 1:6, :, 0:PAD, :] = zero
        v[t, 1:6, :, PAD + ROWS:, :] = zero

    @pl.when(me.s == 0)
    def _():
        @pl.loop(0, TICKS * STEPS)
        def _(k):
            halo[0, k] = jnp.zeros((2, ROWS, 128), jnp.float32)

    @pl.when(me.s == count - 1)
    def _():
        @pl.loop(0, TICKS * STEPS)
        def _(k):
            halo[1, k] = jnp.zeros((2, ROWS, 128), jnp.float32)

    peers = jnp.int32(4)
    for side in range(2):
        peers += len(passers[side]) * (me.s == ends[side]).astype(jnp.int32)
        for passer in passers[side]:
            peers += (me.s == passer).astype(jnp.int32)
    pl.semaphore_wait(barrier, peers)

    def halo_copy(t, j, side):
        lo, hi = BOUNDS[t][j], BOUNDS[t][j + 1]
        planes = pl.ds(2, 2) if side == 0 else pl.ds(0, 2)
        if t == 0:
            src = prior.at[:, planes, pl.ds(lo, hi - lo), :]
        else:
            src = v.at[t - 1, 1:6, planes, pl.ds(PAD + lo, hi - lo), :]
        return pltpu.make_async_remote_copy(
            src_ref=src,
            dst_ref=halo.at[side, pl.ds(STEPS * t, STEPS), :, pl.ds(lo, hi - lo), :],
            send_sem=h_send.at[t, j, side],
            recv_sem=h_recv.at[t, j, side],
            device_id=up if side == 0 else down,
            device_id_type=MESH,
        )

    def passer_of(t, j, side):
        if t == 0:
            return passers[side][0] if j % 2 else None
        return passers[side][(j - 1) % len(passers[side])] if j else None

    def pass_in(t, j, side):
        lo, hi = BOUNDS[t][j], BOUNDS[t][j + 1]
        planes = pl.ds(2 - 2 * side, 2)
        if t == 0:
            src = prior.at[:, planes, pl.ds(lo, hi - lo), :]
        else:
            src = v.at[t - 1, 1:6, planes, pl.ds(PAD + lo, hi - lo), :]
        return pltpu.make_async_remote_copy(
            src_ref=src,
            dst_ref=passing.at[t, :, :, pl.ds(lo, hi - lo), :],
            send_sem=h_send.at[t, j, side],
            recv_sem=p_recv.at[t, j],
            device_id={"space": passer_of(t, j, side)},
            device_id_type=MESH,
        )

    def pass_out(t, j, side):
        lo, hi = BOUNDS[t][j], BOUNDS[t][j + 1]
        return pltpu.make_async_remote_copy(
            src_ref=passing.at[t, :, :, pl.ds(lo, hi - lo), :],
            dst_ref=halo.at[side, pl.ds(STEPS * t, STEPS), :, pl.ds(lo, hi - lo), :],
            send_sem=p_send.at[t, j],
            recv_sem=h_recv.at[t, j, side],
            device_id={"space": ends[1 - side]},
            device_id_type=MESH,
        )

    def forward(t, j):
        for side in range(2):
            @pl.when(me.s == passer_of(t, j, side))
            def _():
                pass_in(t, j, side).wait_recv()
                pass_out(t, j, side).start()

    def wait_forwarded(t, j):
        for side in range(2):
            @pl.when(me.s == passer_of(t, j, side))
            def _():
                pass_out(t, j, side).wait_send()

    def send_halo(t, j):
        roundabout = passer_of(t, j, 0) is not None
        for side, near in ((0, me.s < count - 1), (1, me.s > 0)):
            if roundabout:
                near = near & (me.s != ends[side])

                @pl.when(me.s == ends[side])
                def _():
                    pass_in(t, j, side).start()

            @pl.when(near)
            def _():
                halo_copy(t, j, side).start()

    def wait_halo(t, j):
        @pl.when(me.s > 0)
        def _():
            halo_copy(t, j, 0).wait_recv()

        @pl.when(me.s < count - 1)
        def _():
            halo_copy(t, j, 1).wait_recv()

    def wait_halo_sent(t, j):
        @pl.when(me.s < count - 1)
        def _():
            halo_copy(t, j, 0).wait_send()

        @pl.when(me.s > 0)
        def _():
            halo_copy(t, j, 1).wait_send()

    def state_copy(t, j):
        rows = pl.ds(PAD + BOUNDS[t][j], BOUNDS[t][j + 1] - BOUNDS[t][j])
        return pltpu.make_async_remote_copy(
            src_ref=v.at[t - 1, 5:7, :, rows, :],
            dst_ref=v.at[t, 0:2, :, rows, :],
            send_sem=s_send.at[t - 1, j],
            recv_sem=s_recv.at[t - 1, j],
            device_id=back[0],
            device_id_type=MESH,
        )

    def home_copy(j, level):
        lo, hi = BOUNDS[TICKS][j], BOUNDS[TICKS][j + 1]
        out = (out_prev, out_cur)[level]
        return pltpu.make_async_remote_copy(
            src_ref=v.at[TICKS - 1, 5 + level, :, pl.ds(PAD + lo, hi - lo), :],
            dst_ref=out.at[:, pl.ds(lo, hi - lo), :],
            send_sem=s_send.at[TICKS - 1 + level, j],
            recv_sem=s_recv.at[TICKS - 1 + level, j],
            device_id=home[0],
            device_id_type=MESH,
        )

    for j in range(CHUNKS):
        send_halo(0, j)

    loads[0].wait()
    loads[1].wait()

    @pl.loop(0, ROWS // 8)
    def _(k):
        rows = pl.ds(pl.multiple_of(k * 8, 8), 8)
        scaled = raw[0, :, rows, :] * (TIME_STEP_SQ / 12.0)
        wk[0, :, rows, :] = scaled
        wk[1, :, rows, :] = raw[1, :, rows, :] * (3.0 * TIME_STEP_SQ)
        wk[2, :, rows, :] = 2.0 - 90.0 * scaled

    loads[2].wait()
    loads[3].wait()

    def step_block(t, n, r, size):
        mid = pl.ds(r + PAD, size)
        rows = pl.ds(r, size)
        lane = lax.broadcasted_iota(jnp.int32, (size, 128), 1)
        k = STEPS * t + n
        col = [halo[0, k, 0, rows, :], halo[0, k, 1, rows, :],
               *[v[t, n + 1, z, mid, :] for z in range(4)],
               halo[1, k, 0, rows, :], halo[1, k, 1, rows, :]]
        for z in range(4):
            c = col[z + 2]

            def shifted(off):
                return v[t, n + 1, z, pl.ds(r + PAD + off, size), :]

            def turned(off):
                inside = lane >= off if off > 0 else lane < 128 + off
                return jnp.where(inside, pltpu.roll(c, off % 128, 1), 0.0)

            s1 = (shifted(-1) + shifted(1)) + (col[z + 1] + col[z + 3]) + (turned(-1) + turned(1))
            s2 = (shifted(-2) + shifted(2)) + (col[z] + col[z + 4]) + (turned(-2) + turned(2))
            g = path0[n, z, rows, :] if t == 0 else v[t - 1, n + 1, z, mid, :]
            v[t, n + 2, z, mid, :] = (
                (wk[2, z, rows, :] * c - v[t, n, z, mid, :])
                + wk[0, z, rows, :] * (16.0 * s1 - s2)
                + (wk[1, z, rows, :] * (g * g)) * ((2.0 / 3.0) * g - c)
            )

    def step_rows(t, n, lo, hi):
        if hi <= lo:
            return
        size = 16
        for r in range(lo, hi, size):
            step_block(t, n, r, min(size, hi - r))

    forwards = [(j - FORWARD_AFTER, 0, j) for j in range(1, CHUNKS, 2)]
    for t in range(TICKS):
        bounds = BOUNDS[t]
        sent = 0
        for j in range(CHUNKS):
            event = CHUNKS * t + j
            due = [f for f in forwards if f[0] + FORWARD_AFTER <= event]
            forwards = [f for f in forwards if f not in due]
            for f in due:
                forward(*f[1:])
            if t > 0:
                state_copy(t, j).wait_recv()
            wait_halo(t, j)
            lo, hi = bounds[j], bounds[j + 1]
            for n in range(STEPS):
                lag = LAG * (n + 1)
                step_rows(t, n, max(0, lo - lag), ROWS if hi == ROWS else max(0, hi - lag))
            ready = emitted(t, hi)
            while sent < CHUNKS and BOUNDS[t + 1][sent + 1] <= ready:
                if t + 1 == TICKS:
                    home_copy(sent, 0).start()
                    home_copy(sent, 1).start()
                else:
                    state_copy(t + 1, sent).start()
                    send_halo(t + 1, sent)
                    if sent:
                        forwards.append((event, t + 1, sent))
                sent += 1
    for j in range(CHUNKS):
        home_copy(j, 0).wait_recv()
        home_copy(j, 1).wait_recv()
    for t in range(TICKS):
        for j in range(CHUNKS):
            wait_halo_sent(t, j)
            if passer_of(t, j, 0) is not None:
                wait_forwarded(t, j)
            if t + 1 < TICKS:
                state_copy(t + 1, j).wait_send()
            else:
                home_copy(j, 0).wait_send()
                home_copy(j, 1).wait_send()


def per_device(nz, start_state, prior_path, wave_speed, kerr_coeff):
    any_space = pl.BlockSpec(memory_space=pl.ANY)
    level = jax.ShapeDtypeStruct((4, ROWS, 128), jnp.float32)
    previous, current = pl.pallas_call(
        functools.partial(kernel, nz),
        out_shape=(level, level),
        in_specs=[any_space] * 4,
        out_specs=(any_space, any_space),
        scratch_shapes=[
            pltpu.VMEM((TICKS, 7, 4, ROWS + 2 * PAD, 128), jnp.float32),
            pltpu.VMEM((STEPS, 4, ROWS, 128), jnp.float32),
            pltpu.VMEM((2, TICKS * STEPS, 2, ROWS, 128), jnp.float32),
            pltpu.VMEM((TICKS, STEPS, 2, ROWS, 128), jnp.float32),
            pltpu.VMEM((3, 4, ROWS, 128), jnp.float32),
            pltpu.VMEM((2, 4, ROWS, 128), jnp.float32),
            pltpu.SemaphoreType.DMA((TICKS, CHUNKS, 2)),
            pltpu.SemaphoreType.DMA((TICKS, CHUNKS, 2)),
            pltpu.SemaphoreType.DMA((TICKS + 1, CHUNKS)),
            pltpu.SemaphoreType.DMA((TICKS + 1, CHUNKS)),
            pltpu.SemaphoreType.DMA((TICKS, CHUNKS)),
            pltpu.SemaphoreType.DMA((TICKS, CHUNKS)),
            pltpu.SemaphoreType.DMA((4,)),
        ],
        compiler_params=pltpu.CompilerParams(
            collective_id=0, has_side_effects=True, vmem_limit_bytes=62 << 20
        ),
        name="relaxation",
    )(start_state[0], prior_path[0], wave_speed, kerr_coeff)
    return jnp.stack([previous, current], 0)[None]


def solution(mesh):
    nz = mesh.shape["space"] // 4
    return jax.shard_map(
        functools.partial(per_device, nz),
        mesh=mesh,
        in_specs=(
            P("iter", None, "space", None, None),
            P("iter", None, "space", None, None),
            P("space", None, None),
            P("space", None, None),
        ),
        out_specs=P("iter", None, "space", None, None),
        check_vma=False,
    )
```
